32 devices in a mesh: ctx: 8 (over z, x), head: 4 (over y, core).
Axes of the slice: x: 2, y: 2, z: 4, core: 2. Of those that a mesh axis runs over, the one named last changes fastest.
Arguments:
- q_win: bfloat16 [2048, 8192], P('ctx', 'head'), may hold values from -64 to 64
- k_win: bfloat16 [2048, 2048], P('ctx', 'head'), may hold values from -6 to 6
- v_win: bfloat16 [2048, 2048], P('ctx', 'head'), may hold values from -5 to 5
- q_lin: bfloat16 [2048, 8192], P('ctx', 'head'), may hold values from -5 to 5
- k_lin: bfloat16 [2048, 2048], P('ctx', 'head'), may hold values from -5 to 5
- v_lin: bfloat16 [2048, 2048], P('ctx', 'head'), may hold values from -5 to 5
- level_table: float32 [64, 64, 4], P(None, 'head'), may hold values from 0.05 to 0.6
- level_index: int32 [2048], P('ctx'), may hold values from 0 to 63
- q_cross: bfloat16 [2048, 8192], P('ctx', 'head'), may hold values from -64 to 64
- k_shared: bfloat16 [2048, 2048], P('ctx', 'head'), may hold values from -6 to 6
- v_shared: bfloat16 [2048, 2048], P('ctx', 'head'), may hold values from -5 to 5
- head_gain: float32 [64], P('head'), may hold values from 0.5 to 13.5
Outputs:
- attended: bfloat16 [2048, 8192], P('ctx', 'head')
The draws below stay inside these ranges and needn't reach their ends.
All inputs are finite; a program needn't handle non-finite values.
Results may differ from the reference program's by a relative error of at most 0.008.
Values may be sent and summed in bfloat16 or wider, within the bound.
No kernel may reach another device: no remote copies, remote signals or barrier semaphores. Data moves between devices by JAX's collectives and lax.ppermute only.
A program may use at most 192 MiB of HBM per device.

```python
import math
import jax
import jax.numpy as jnp
import numpy as np
from jax import lax

QH = 64
KVH = 16
HEAD_SIZE = 128
W = 512
TOKENS_PER_SHARD = 256
TABLE = 64
TOKENS = 2048
LEVELS = 4
N_CTX = 8


def drawn_pair(key, salt_value, scale_q):
    base_key = jax.random.fold_in(key, salt_value)
    key_q, key_k = jax.random.split(base_key, 2)
    query_matrix = jnp.clip(jax.random.normal(key_q, (TOKENS, QH, HEAD_SIZE), jnp.float32), -4.0, 4.0) * scale_q
    key_row_slice = jnp.clip(jax.random.normal(key_k, (TOKENS, KVH, HEAD_SIZE), jnp.float32), -4.0, 4.0)
    query_matrix = jnp.clip(query_matrix, -64.0, 64.0).reshape(TOKENS, QH * HEAD_SIZE)
    key_row_slice = jnp.clip(key_row_slice, -6.0, 6.0).reshape(TOKENS, KVH * HEAD_SIZE)
    return (query_matrix, key_row_slice)


def draw_q_win(key, part):
    return drawn_pair(key, 11, 2.5)[0].astype(jnp.bfloat16)


def draw_k_win(key, part):
    return drawn_pair(key, 11, 2.5)[1].astype(jnp.bfloat16)


def draw_q_cross(key, part):
    return drawn_pair(key, 23, 2.5)[0].astype(jnp.bfloat16)


def draw_k_shared(key, part):
    return drawn_pair(key, 23, 2.5)[1].astype(jnp.bfloat16)


def draw_head_gain(key, part):
    base_key = jax.random.fold_in(key, 37)
    spread = jnp.exp(jax.random.uniform(base_key, (QH,), jnp.float32, jnp.log(0.5), jnp.log(1.5)))
    ramp_up = jnp.arange(QH, dtype=jnp.float32) / (QH - 1)
    return spread * 3.0 ** ramp_up


def place_ends(values, rng, smallest, largest):
    extent = values.shape
    index_at = [jax.random.randint(jax.random.fold_in(rng, axis), (), 0, extent[axis]) for axis in range(len(extent))]
    values = values.at[tuple(index_at)].set(smallest)
    longest = extent.index(max(extent))
    index_at[longest] = (index_at[longest] + 1) % extent[longest]
    return values.at[tuple(index_at)].set(largest)


def level_of(own_key, dims, shards, low, top_value):
    def one(position, shards_of):
        steps = jax.random.uniform(jax.random.fold_in(jax.random.fold_in(own_key, 6), position), (shards_of,), jnp.float32, low / len(shards), top_value / len(shards))
        return jnp.repeat(jnp.exp(steps), dims[position] // shards_of).reshape((-1,) + (1,) * (len(dims) - position - 1))

    factor_of = one(*shards[0])
    for cut in shards[1:]:
        factor_of = factor_of * one(*cut)
    return factor_of


def noise(own_key, dims, scale, most, cuts=(), held_as=jnp.bfloat16):
    gain = level_of(own_key, dims, cuts, -0.22, 0.18) if cuts else 1.0
    values = jax.random.normal(own_key, dims, jnp.float32) * scale * gain
    return jnp.minimum(jnp.maximum(values, -most), most).astype(held_as)


def setup_inputs(seed: int = 0) -> dict:
    streams_of = jax.random.split(jax.random.key(seed), 13)
    q_win = draw_q_win(jax.random.fold_in(streams_of[12], 71), 0)
    k_win = draw_k_win(jax.random.fold_in(streams_of[12], 71), 0)
    v_win = noise(streams_of[2], (TOKENS, KVH * HEAD_SIZE), 1.0, 5.0, ((0, 8), (1, 4)))
    q_lin = noise(streams_of[3], (TOKENS, QH * HEAD_SIZE), 1.0, 5.0, ((0, 8), (1, 4)))
    k_lin = noise(streams_of[4], (TOKENS, KVH * HEAD_SIZE), 1.0, 5.0, ((0, 8), (1, 4)))
    v_lin = noise(streams_of[5], (TOKENS, KVH * HEAD_SIZE), 1.0, 5.0, ((0, 8), (1, 4)))
    level_table = jnp.clip(jnp.exp(math.log(0.6) - 2.4849067 * jax.random.uniform(streams_of[6], (TABLE, QH, LEVELS), jnp.float32) ** level_of(streams_of[6], (TABLE, QH, LEVELS), ((1, 4),), -0.2, 0.2)), 0.05, 0.6)
    level_index = place_ends(jax.random.randint(streams_of[7], (TOKENS,), 0, TABLE), jax.random.fold_in(streams_of[7], 1), 0, TABLE - 1).astype(jnp.int32)
    q_cross = draw_q_cross(jax.random.fold_in(streams_of[12], 71), 0)
    k_shared = draw_k_shared(jax.random.fold_in(streams_of[12], 71), 0)
    v_shared = noise(streams_of[10], (TOKENS, KVH * HEAD_SIZE), 1.0, 5.0, ((0, 8), (1, 4)))
    head_gain = draw_head_gain(jax.random.fold_in(streams_of[12], 71), 0)
    return dict(q_win=q_win, k_win=k_win, v_win=v_win, q_lin=q_lin, k_lin=k_lin, v_lin=v_lin, level_table=level_table, level_index=level_index, q_cross=q_cross, k_shared=k_shared, v_shared=v_shared, head_gain=head_gain)


exact_precision_flag = lax.Precision.HIGHEST

def softmax_rows(query_rows, key_row_slice, value_rows, query_pos, key_pos, horizon):
    count_q = query_rows.shape[0]
    count_k = key_row_slice.shape[0]
    per_group = QH // KVH
    allowed = (key_pos[None, :] <= query_pos[:, None]) & (key_pos[None, :] > query_pos[:, None] - horizon)
    query_matrix = query_rows.reshape(count_q, KVH, per_group, HEAD_SIZE).transpose(1, 2, 0, 3).astype(jnp.float32)
    key_heads = key_row_slice.reshape(count_k, KVH, HEAD_SIZE).transpose(1, 0, 2).astype(jnp.float32)
    value_heads = value_rows.reshape(count_k, KVH, HEAD_SIZE).transpose(1, 0, 2).astype(jnp.float32)

    def one_group(members):
        group_q, group_k, group_v = members
        attention_scores = jnp.einsum('rtd,sd->rts', group_q, group_k, precision=exact_precision_flag) * HEAD_SIZE ** (-0.5)
        attention_scores = jnp.where(allowed[None], attention_scores, -1e+30)
        highest = lax.optimization_barrier(jnp.max(attention_scores, axis=-1, keepdims=True))
        weights = jnp.where(allowed[None], jnp.exp(attention_scores - highest), 0.0)
        totals = lax.optimization_barrier(jnp.sum(weights, axis=-1, keepdims=True))
        rounded_values = lax.optimization_barrier(weights.astype(jnp.bfloat16)).astype(jnp.float32)
        return jnp.einsum('rts,sd->rtd', rounded_values, group_v, precision=exact_precision_flag) / totals
    result = lax.map(one_group, (query_matrix, key_heads, value_heads))
    return result.transpose(2, 0, 1, 3).reshape(count_q, QH * HEAD_SIZE)

def causal_pass(query_all, key_all, value_all, horizon):
    block_rows = 512 if TOKENS % 512 == 0 else TOKENS_PER_SHARD
    outputs = []
    for start_row in range(0, TOKENS, block_rows):
        first_key = max(0, start_row - horizon + 1)
        end_row = start_row + block_rows
        outputs.append(softmax_rows(query_all[start_row:end_row], key_all[first_key:end_row], value_all[first_key:end_row], jnp.arange(start_row, end_row, dtype=jnp.int32), jnp.arange(first_key, end_row, dtype=jnp.int32), horizon))
    return jnp.concatenate(outputs, axis=0)

def log_linear(q_lin, k_lin, v_lin, level_table, level_index):
    blocks = N_CTX
    per_group = QH // KVH
    query_matrix = q_lin.reshape(blocks, TOKENS_PER_SHARD, KVH, per_group, HEAD_SIZE).astype(jnp.float32)
    key_blocks = k_lin.reshape(blocks, TOKENS_PER_SHARD, KVH, HEAD_SIZE).astype(jnp.float32)
    value_blocks = v_lin.reshape(blocks, TOKENS_PER_SHARD, KVH, HEAD_SIZE).astype(jnp.float32)
    causal = jnp.arange(TOKENS_PER_SHARD)[:, None] >= jnp.arange(TOKENS_PER_SHARD)[None, :]

    def inner_block(members):
        fenwick_block_query, fenwick_block_key, fenwick_block_value = members
        attention_scores = jnp.einsum('ufjn,efn->fjue', fenwick_block_query, fenwick_block_key, precision=exact_precision_flag) * (HEAD_SIZE * TOKENS_PER_SHARD) ** (-0.5)
        attention_scores = jnp.where(causal, attention_scores, 0.0)
        rounded_values = lax.optimization_barrier(attention_scores.astype(jnp.bfloat16)).astype(jnp.float32)
        return jnp.einsum('koyw,wku->ykou', rounded_values, fenwick_block_value, precision=exact_precision_flag)
    inside = lax.map(inner_block, (query_matrix, key_blocks, value_blocks))
    states = jnp.einsum('nsgd,nsge->ngde', key_blocks, value_blocks, precision=exact_precision_flag)
    level_weights = level_table[level_index].reshape(blocks, TOKENS_PER_SHARD, KVH, per_group, LEVELS)
    mixed_out = level_weights[..., 0:1] * inside
    block_ids = np.arange(blocks)
    for level_no in range(1, LEVELS):
        half_span = 2 ** (level_no - 1)
        grouped = states.reshape(blocks // half_span, half_span, KVH, HEAD_SIZE, HEAD_SIZE).sum(axis=1)
        chosen = np.maximum((block_ids >> level_no - 1) - 1, 0)
        present = block_ids >> level_no - 1 & 1 == 1
        bucket = jnp.where(jnp.asarray(present)[:, None, None, None], grouped[chosen], 0.0)
        readout = jnp.einsum('ntgrd,ngde->ntgre', query_matrix, bucket, precision=exact_precision_flag)
        readout = readout * (HEAD_SIZE * TOKENS_PER_SHARD * half_span) ** (-0.5)
        mixed_out = mixed_out + level_weights[..., level_no:level_no + 1] * readout
    return mixed_out.reshape(TOKENS, QH * HEAD_SIZE)

def reference(q_win, k_win, v_win, q_lin, k_lin, v_lin, level_table, level_index, q_cross, k_shared, v_shared, head_gain):
    window_out = causal_pass(q_win, k_win, v_win, W)
    linear_out = log_linear(q_lin, k_lin, v_lin, level_table, level_index)
    cross_out = causal_pass(q_cross, k_shared, v_shared, TOKENS + 1)
    combined = (window_out + linear_out + cross_out).reshape(TOKENS, QH, HEAD_SIZE) * head_gain[None, :, None]
    mean_square = lax.optimization_barrier(jnp.sum(combined * combined, axis=(1, 2))) / (QH * HEAD_SIZE)
    scaled = combined * lax.rsqrt(mean_square + 1e-06)[:, None, None]
    return scaled.reshape(TOKENS, QH * HEAD_SIZE).astype(jnp.bfloat16)
```

```python
import functools
import math

import jax
import jax.numpy as jnp
from jax import lax
from jax.experimental import pallas as pl
from jax.experimental.pallas import tpu as pltpu
from jax.sharding import PartitionSpec as P

QH = 64
HEAD_SIZE = 128
W = 512
LANES = 128
far_below = -1e30
exact = lax.Precision.HIGHEST
nt_dims = (((1,), (1,)), ((), ()))


def shifted(value, axis, steps):
    count = lax.axis_size(axis)
    first, last = (max(0, -steps), min(count, count - steps))
    return lax.ppermute(value, axis, [(source, source + steps) for source in range(first, last)])


def partner(block, axis, apart):
    count = lax.axis_size(axis)
    route = []
    for low in range(count):
        high = low | 1 << apart
        if high != low and high < count:
            route += [(low, high), (high, low)]
    return lax.ppermute(block, axis, route)


def scores_of(q, k):
    return lax.dot_general(q, k, nt_dims, preferred_element_type=jnp.float32)


def with_ones(v):
    return jnp.concatenate([v, jnp.ones(v.shape, v.dtype)], axis=1)


def lower_mask(s, first, last):
    rows = s.shape[0]
    row = lax.broadcasted_iota(jnp.int32, (rows, rows), 0)
    col = lax.broadcasted_iota(jnp.int32, (rows, rows), 1)
    parts = []
    width = s.shape[1]
    if first:
        parts.append(jnp.where(col > row, s[:, :rows], far_below))
    middle = s[:, rows if first else 0 : width - rows if last else width]
    if middle.shape[1]:
        parts.append(middle)
    if last:
        parts.append(jnp.where(col <= row, s[:, width - rows :], far_below))
    return parts[0] if len(parts) == 1 else jnp.concatenate(parts, axis=1)


def softmax_part(s, v_ext, unit):
    m = jnp.max(s, axis=1, keepdims=True) * unit
    p = jnp.exp2(s * unit - m)
    pv = jnp.dot(p.astype(jnp.bfloat16), v_ext, preferred_element_type=jnp.float32)
    return m, pv


UNIT = HEAD_SIZE ** (-0.5) * math.log2(math.e)


def local_kernel(heads, tile, q_ref, kv_ref, acc_ref, st_ref):
    d = HEAD_SIZE
    rows = q_ref.shape[0]
    k = kv_ref[0]
    v_ext = with_ones(kv_ref[1])
    lane = lax.broadcasted_iota(jnp.int32, (tile, LANES), 1)
    for t in range(0, rows, tile):
        st = jnp.zeros((tile, LANES), jnp.float32)
        for h in range(heads):
            q = q_ref[t : t + tile, h * d : (h + 1) * d]
            s = lower_mask(scores_of(q, k[: t + tile]), False, True)
            m, pv = softmax_part(s, v_ext[: t + tile], UNIT)
            acc_ref[t : t + tile, h * d : (h + 1) * d] = pv[:, :d]
            st = jnp.where(lane == 2 * h, m, st)
            st = jnp.where(lane == 2 * h + 1, pv[:, d:], st)
        st_ref[0, t : t + tile] = st


def piece_body(heads, tile, q_ref, k, v_ext, acc_ref, st_ref, emit):
    d = HEAD_SIZE
    rows = q_ref.shape[0]
    for t in range(0, rows, tile):
        old = st_ref[0, t : t + tile]
        for h in range(heads):
            q = q_ref[t : t + tile, h * d : (h + 1) * d]
            s = scores_of(q, k)
            m_old = old[:, 2 * h : 2 * h + 1]
            l_old = old[:, 2 * h + 1 : 2 * h + 2]
            m = jnp.maximum(jnp.max(s, axis=1, keepdims=True) * UNIT, m_old)
            p = jnp.exp2(s * UNIT - m)
            pv = jnp.dot(p.astype(jnp.bfloat16), v_ext, preferred_element_type=jnp.float32)
            fade = jnp.exp2(m_old - m)
            acc = acc_ref[t : t + tile, h * d : (h + 1) * d] * fade + pv[:, :d]
            emit(t, h, m, l_old * fade + pv[:, d:], acc)


def piece_kernel(heads, tile, blocks, at_ref, q_ref, *refs):
    kv_refs = refs[:blocks]
    acc_ref, st_ref, acc_out, st_out = refs[blocks:]
    lane = lax.broadcasted_iota(jnp.int32, (tile, LANES), 1)
    live = at_ref[0] != 0

    @pl.when(live)
    def _():
        k = jnp.concatenate([r[0] for r in kv_refs], axis=0)
        v_ext = with_ones(jnp.concatenate([r[1] for r in kv_refs], axis=0))
        held = {}

        def emit(t, h, m, l, acc):
            acc_out[t : t + tile, h * HEAD_SIZE : (h + 1) * HEAD_SIZE] = acc
            st = held.get("st", jnp.zeros((tile, LANES), jnp.float32)) if h else jnp.zeros(
                (tile, LANES), jnp.float32
            )
            st = jnp.where(lane == 2 * h, m, st)
            held["st"] = jnp.where(lane == 2 * h + 1, l, st)
            if h == heads - 1:
                st_out[0, t : t + tile] = held["st"]

        piece_body(heads, tile, q_ref, k, v_ext, acc_ref, st_ref, emit)

    @pl.when(jnp.logical_not(live))
    def _():
        acc_out[...] = acc_ref[...]
        st_out[...] = st_ref[...]


def last_kernel(heads, tile, blocks, at_ref, q_ref, *refs):
    kv_refs = refs[:blocks]
    acc_ref, st_ref, side_ref, gain_ref, comb_ref, sq_ref = refs[blocks:]
    d = HEAD_SIZE
    live = at_ref[0] != 0
    rows = q_ref.shape[0]

    @pl.when(pl.program_id(0) == 0)
    def _():
        sq_ref[...] = jnp.zeros_like(sq_ref)

    def put(t, h, l, acc):
        cols = slice(h * d, (h + 1) * d)
        comb_ref[t : t + tile, cols] = gain_ref[0:1, cols] * (
            side_ref[t : t + tile, cols] + acc / l
        )

    @pl.when(live)
    def _():
        k = jnp.concatenate([r[0] for r in kv_refs], axis=0)
        v_ext = with_ones(jnp.concatenate([r[1] for r in kv_refs], axis=0))
        piece_body(
            heads, tile, q_ref, k, v_ext, acc_ref, st_ref, lambda t, h, m, l, acc: put(t, h, l, acc)
        )

    @pl.when(jnp.logical_not(live))
    def _():
        for t in range(0, rows, tile):
            old = st_ref[0, t : t + tile]
            for h in range(heads):
                put(
                    t,
                    h,
                    old[:, 2 * h + 1 : 2 * h + 2],
                    acc_ref[t : t + tile, h * d : (h + 1) * d],
                )

    total = jnp.zeros((rows, d), jnp.float32)
    for h in range(heads):
        c = comb_ref[:, h * d : (h + 1) * d]
        total = total + c * c
    sq_ref[...] += lax.dot_general(
        jnp.ones((8, d), jnp.float32), total, nt_dims, precision=exact
    )


def side_kernel(heads, tile, behind, levels, at_ref, qw_ref, own_ref, *refs):
    d = HEAD_SIZE
    back = refs[:behind]
    other_ref, ql_ref, kl_ref, vl_ref = refs[behind : behind + 4]
    buckets = refs[behind + 4 : behind + 4 + levels]
    idx_ref, table_ref, out_ref = refs[behind + 4 + levels :]
    rows = qw_ref.shape[0]
    here = at_ref[0]
    pick = at_ref[1] != 0

    entries = table_ref.shape[1]
    one_hot = (
        idx_ref[...] == lax.broadcasted_iota(jnp.int32, (rows, entries), 1)
    ).astype(jnp.float32)
    weights = jnp.dot(one_hot, table_ref[0], precision=exact, preferred_element_type=jnp.float32)

    kl = kl_ref[...]
    vl = vl_ref[...]
    wide = jnp.concatenate([b[0] for b in buckets], axis=1)
    row = lax.broadcasted_iota(jnp.int32, (tile, tile), 0)
    col = lax.broadcasted_iota(jnp.int32, (tile, tile), 1)
    for t in range(0, rows, tile):
        for h in range(heads):
            cols = slice(h * d, (h + 1) * d)
            q = ql_ref[t : t + tile, cols]
            a = scores_of(q, kl[: t + tile]) * (d * rows) ** (-0.5)
            tail = jnp.where(col <= row, a[:, t:], 0.0)
            a = jnp.concatenate([a[:, :t], tail], axis=1) if t else tail
            intra = jnp.dot(
                a.astype(jnp.bfloat16), vl[: t + tile], preferred_element_type=jnp.float32
            )
            first = h * (levels + 1)
            out = weights[t : t + tile, first : first + 1] * intra
            read = jnp.dot(q, wide, preferred_element_type=jnp.float32)
            for level in range(1, levels + 1):
                present = ((here >> (level - 1)) & 1).astype(jnp.float32)
                scale = (d * rows * 2 ** (level - 1)) ** (-0.5) * present
                out = out + (weights[t : t + tile, first + level : first + level + 1] * scale) * read[
                    :, (level - 1) * d : level * d
                ]
            out_ref[t : t + tile, cols] = out

    near = jnp.where(pick, back[-1][...], other_ref[...])
    pieces = [r[...] for r in back[:-1]] + [near, own_ref[...]]
    k = jnp.concatenate([p[0] for p in pieces], axis=0)
    v_ext = with_ones(jnp.concatenate([p[1] for p in pieces], axis=0))

    def window(general):
        for t in range(0, rows, tile):
            start = 0 if general else behind * rows + t - W
            stop = behind * rows + rows if general else behind * rows + t + tile
            for h in range(heads):
                cols = slice(h * d, (h + 1) * d)
                q = qw_ref[t : t + tile, cols]
                s = scores_of(q, k[start:stop])
                if general:
                    at_row = behind * rows + t + lax.broadcasted_iota(jnp.int32, s.shape, 0)
                    at_col = lax.broadcasted_iota(jnp.int32, s.shape, 1)
                    allowed = (at_col <= at_row) & (at_col > at_row - W)
                    allowed = allowed & (at_col >= (behind - here) * rows)
                    s = jnp.where(allowed, s, far_below)
                else:
                    s = lower_mask(s, True, True)
                m, pv = softmax_part(s, v_ext[start:stop], UNIT)
                out_ref[t : t + tile, cols] += pv[:, :d] / pv[:, d:]

    if (behind * rows) == W and rows % tile == 0:

        @pl.when(here >= behind)
        def _():
            window(False)

        @pl.when(here < behind)
        def _():
            window(True)

    else:
        window(True)


def norm_kernel(columns, comb_ref, sq_ref, out_ref):
    sums = jnp.transpose(sq_ref[...])[:, 0:1]
    out_ref[...] = (comb_ref[...] * lax.rsqrt(sums / columns + 1e-06)).astype(out_ref.dtype)


def per_device(
    q_win,
    k_win,
    v_win,
    q_lin,
    k_lin,
    v_lin,
    level_table,
    level_index,
    q_cross,
    k_shared,
    v_shared,
    head_gain,
):
    d = HEAD_SIZE
    rows = q_win.shape[0]
    groups = k_win.shape[1] // d
    heads = q_win.shape[1] // k_win.shape[1]
    wide = heads * d
    count = lax.axis_size("ctx")
    levels = count.bit_length() - 1
    tile = 128
    here = lax.axis_index("ctx").astype(jnp.int32)
    side_bit = here & 1
    deep = here >> 1
    behind = -(-W // rows)

    f32 = jnp.float32
    q_spec = pl.BlockSpec((rows, wide), lambda g, *_: (0, g))
    k_spec = pl.BlockSpec((rows, d), lambda g, *_: (0, g))
    kv_spec = pl.BlockSpec((2, rows, d), lambda g, *_: (0, 0, g))
    st_spec = pl.BlockSpec((1, rows, LANES), lambda g, *_: (g, 0, 0))
    acc_type = jax.ShapeDtypeStruct((rows, groups * wide), f32)
    st_type = jax.ShapeDtypeStruct((groups, rows, LANES), f32)
    params = pltpu.CompilerParams(dimension_semantics=("arbitrary",))

    def cost(keys, extra=0):
        pairs = rows * keys * groups * heads
        return pl.CostEstimate(
            flops=4 * pairs * d,
            transcendentals=pairs,
            bytes_accessed=2 * rows * groups * wide * 5 + extra,
        )

    def run_local(kv):
        return pl.pallas_call(
            functools.partial(local_kernel, heads, tile),
            grid=(groups,),
            in_specs=[q_spec, kv_spec],
            out_specs=[q_spec, st_spec],
            out_shape=[acc_type, st_type],
            compiler_params=params,
            cost_estimate=cost(rows),
            name="cross_local",
        )(q_cross, kv)

    def run_piece(live, kvs, acc, st):
        n = len(kvs)
        return pl.pallas_call(
            functools.partial(piece_kernel, heads, tile, n),
            grid_spec=pltpu.PrefetchScalarGridSpec(
                num_scalar_prefetch=1,
                grid=(groups,),
                in_specs=[q_spec] + [kv_spec] * n + [q_spec, st_spec],
                out_specs=[q_spec, st_spec],
            ),
            out_shape=[acc_type, st_type],
            compiler_params=params,
            cost_estimate=cost(n * rows),
            name="cross_piece",
        )(live.astype(jnp.int32).reshape(1), q_cross, *kvs, acc, st)

    def run_last(live, kvs, acc, st, side, gain):
        n = len(kvs)
        return pl.pallas_call(
            functools.partial(last_kernel, heads, tile, n),
            grid_spec=pltpu.PrefetchScalarGridSpec(
                num_scalar_prefetch=1,
                grid=(groups,),
                in_specs=[q_spec]
                + [kv_spec] * n
                + [q_spec, st_spec, q_spec, pl.BlockSpec((1, wide), lambda g, *_: (0, g))],
                out_specs=[q_spec, pl.BlockSpec((8, rows), lambda g, *_: (0, 0))],
            ),
            out_shape=[acc_type, jax.ShapeDtypeStruct((8, rows), f32)],
            compiler_params=params,
            cost_estimate=cost(n * rows),
            name="cross_last",
        )(live.astype(jnp.int32).reshape(1), q_cross, *kvs, acc, st, side, gain)

    def run_side(own, back, other, pick, buckets, index, table):
        one = pl.BlockSpec((1, d, d), lambda g, *_: (g, 0, 0))
        entries, per = table.shape[1:]
        return pl.pallas_call(
            functools.partial(side_kernel, heads, tile, behind, levels),
            grid_spec=pltpu.PrefetchScalarGridSpec(
                num_scalar_prefetch=1,
                grid=(groups,),
                in_specs=[q_spec, kv_spec]
                + [kv_spec] * behind
                + [kv_spec, q_spec, k_spec, k_spec]
                + [one] * levels
                + [
                    pl.BlockSpec((rows, 1), lambda g, *_: (0, 0)),
                    pl.BlockSpec((1, entries, per), lambda g, *_: (g, 0, 0)),
                ],
                out_specs=q_spec,
            ),
            out_shape=acc_type,
            compiler_params=params,
            cost_estimate=cost((behind + 2) * rows),
            name="side",
        )(
            jnp.stack([here, pick.astype(jnp.int32)]),
            q_win,
            own,
            *back,
            other,
            q_lin,
            k_lin,
            v_lin,
            *buckets,
            index,
            table,
        )

    shared = jnp.stack([k_shared, v_shared])
    near = jnp.stack([k_win, v_win])
    fixed = count == 8 and behind == 2

    state = jnp.einsum(
        "tgd,tge->gde",
        k_lin.reshape(rows, groups, d),
        v_lin.reshape(rows, groups, d),
        preferred_element_type=f32,
    )
    buckets = []
    for level in range(levels):
        arrived = partner(state.astype(jnp.bfloat16), "ctx", level)
        buckets.append(arrived)
        state = state + arrived.astype(f32)
    index = level_index.reshape(rows, 1)
    table = level_table.reshape(level_table.shape[0], groups, -1).transpose(1, 0, 2)
    gain = jnp.repeat(head_gain, d).reshape(1, -1)

    if fixed:
        sides = [(2 * i, 2 * i + 1) for i in range(count // 2)]
        z1 = shifted(shared, "ctx", 2)
        x0 = partner(shared, "ctx", 0)
        z3 = shifted(shared, "ctx", 6)
        back2 = shifted(near, "ctx", 2)
        from_side = lax.ppermute(near, "ctx", sides)
        x1 = partner(z1, "ctx", 0)
        z2 = shifted(z1, "ctx", 2)
        from_back = lax.ppermute(back2, "ctx", [(b, a) for a, b in sides])
        x3 = partner(z3, "ctx", 0)
        x2 = partner(z2, "ctx", 0)
        back, other, pick = [back2, from_side], from_back, side_bit == 1
    else:
        back = [shifted(near, "ctx", step) for step in range(behind, 0, -1)]
        other, pick = back[-1], side_bit == side_bit

    acc, st = run_local(shared)
    side = run_side(near, back, other, pick, buckets, index, table)
    if fixed:
        acc, st = run_piece(side_bit == 1, [x0], acc, st)
        acc, st = run_piece(deep >= 1, [z1, x1], acc, st)
        acc, st = run_piece(deep >= 3, [z3, x3], acc, st)
        comb, sq = run_last(deep >= 2, [z2, x2], acc, st, side, gain)
    else:
        every = lax.all_gather(shared, "ctx", axis=0, tiled=False)

        def step(source, carried):
            return tuple(run_piece(source < here, [every[source]], *carried))

        acc, st = lax.fori_loop(0, count - 2, step, (acc, st))
        comb, sq = run_last(here > count - 2, [every[count - 2]], acc, st, side, gain)

    sq = lax.psum(sq, "head")
    return pl.pallas_call(
        functools.partial(norm_kernel, QH * d),
        grid=(groups,),
        in_specs=[q_spec, pl.BlockSpec((8, rows), lambda g: (0, 0))],
        out_specs=q_spec,
        out_shape=jax.ShapeDtypeStruct((rows, groups * wide), jnp.bfloat16),
        compiler_params=params,
        name="norm",
    )(comb, sq)


def solution(mesh):
    return jax.shard_map(
        per_device,
        mesh=mesh,
        in_specs=(
            P("ctx", "head"),
            P("ctx", "head"),
            P("ctx", "head"),
            P("ctx", "head"),
            P("ctx", "head"),
            P("ctx", "head"),
            P(None, "head", None),
            P("ctx"),
            P("ctx", "head"),
            P("ctx", "head"),
            P("ctx", "head"),
            P("head"),
        ),
        out_specs=P("ctx", "head"),
        check_vma=False,
    )
```

```python
import functools
import math

import jax
import jax.numpy as jnp
from jax import lax
from jax.experimental import pallas as pl
from jax.experimental.pallas import tpu as pltpu
from jax.sharding import PartitionSpec as P


QH = 64
HEAD_SIZE = 128
W = 512
LANES = 128
far_below = -1e30
exact = lax.Precision.HIGHEST
nt_dims = (((1,), (1,)), ((), ()))


def shifted(value, axis, steps):
    count = lax.axis_size(axis)
    first, last = (max(0, -steps), min(count, count - steps))
    return lax.ppermute(value, axis, [(source, source + steps) for source in range(first, last)])


def partner(block, axis, apart):
    count = lax.axis_size(axis)
    route = []
    for low in range(count):
        high = low | 1 << apart
        if high != low and high < count:
            route += [(low, high), (high, low)]
    return lax.ppermute(block, axis, route)


def scores_of(q, k):
    return lax.dot_general(q, k, nt_dims, preferred_element_type=jnp.float32)


def with_ones(v):
    return jnp.concatenate([v, jnp.ones(v.shape, v.dtype)], axis=1)


def lower_mask(s, first, last):
    rows = s.shape[0]
    row = lax.broadcasted_iota(jnp.int32, (rows, rows), 0)
    col = lax.broadcasted_iota(jnp.int32, (rows, rows), 1)
    parts = []
    width = s.shape[1]
    if first:
        parts.append(jnp.where(col > row, s[:, :rows], far_below))
    middle = s[:, rows if first else 0 : width - rows if last else width]
    if middle.shape[1]:
        parts.append(middle)
    if last:
        parts.append(jnp.where(col <= row, s[:, width - rows :], far_below))
    return parts[0] if len(parts) == 1 else jnp.concatenate(parts, axis=1)


UNIT = HEAD_SIZE ** (-0.5) * math.log2(math.e)
VMEM = pl.BlockSpec(memory_space=pltpu.VMEM)
SMEM = pl.BlockSpec(memory_space=pltpu.SMEM)
TILE = 128


def span(g, size, at=0):
    return pl.ds(pl.multiple_of(g * size + at, LANES), HEAD_SIZE)


def each_group(groups, body):
    lax.fori_loop(0, groups, lambda g, c: (body(g), c)[1], 0)


def pair(ref, g):
    cols = span(g, HEAD_SIZE)
    return ref[0, :, cols], ref[1, :, cols]


def joined(blocks):
    k = jnp.concatenate([b[0] for b in blocks], axis=0)
    v = jnp.concatenate([b[1] for b in blocks], axis=0)
    return k, with_ones(v)


def pack_kernel(k_ref, v_ref, out_ref):
    out_ref[0] = k_ref[...]
    out_ref[1] = v_ref[...]


def state_kernel(k_ref, v_ref, wide_ref, half_ref):
    for g in range(wide_ref.shape[0]):
        cols = slice(g * HEAD_SIZE, (g + 1) * HEAD_SIZE)
        state = lax.dot_general(
            k_ref[:, cols],
            v_ref[:, cols],
            (((0,), (0,)), ((), ())),
            preferred_element_type=jnp.float32,
        )
        wide_ref[g] = state
        half_ref[g] = state.astype(half_ref.dtype)


def local_kernel(heads, groups, q_ref, kv_ref, acc_ref, m_ref, l_ref):
    d = HEAD_SIZE
    rows = q_ref.shape[0]

    def body(g):
        k, v_ext = joined([pair(kv_ref, g)])
        for h in range(heads):
            cols = span(g, heads * d, h * d)
            for t in range(0, rows, TILE):
                at = slice(t, t + TILE)
                s = lower_mask(scores_of(q_ref[at, cols], k[: t + TILE]), False, True)
                m = jnp.max(s, axis=1, keepdims=True) * UNIT
                p = jnp.exp2(s * UNIT - m)
                pv = jnp.dot(
                    p.astype(jnp.bfloat16), v_ext[: t + TILE], preferred_element_type=jnp.float32
                )
                acc_ref[at, cols] = pv[:, :d]
                l_ref[at, cols] = pv[:, d:]
                m_ref[at, cols] = jnp.broadcast_to(m, (TILE, d))

    each_group(groups, body)


def extend(q_ref, acc_ref, m_ref, l_ref, at, cols, k, v_ext):
    d = HEAD_SIZE
    s = scores_of(q_ref[at, cols], k)
    m_old = m_ref[at, cols]
    m = jnp.maximum(jnp.max(s, axis=1, keepdims=True) * UNIT, m_old)
    p = jnp.exp2(s * UNIT - jnp.concatenate([m] * (s.shape[1] // d), axis=1))
    pv = jnp.dot(p.astype(jnp.bfloat16), v_ext, preferred_element_type=jnp.float32)
    fade = jnp.exp2(m_old - m)
    return (
        acc_ref[at, cols] * fade + pv[:, :d],
        m,
        l_ref[at, cols] * fade + pv[:, d:],
    )


def piece_kernel(heads, groups, lives, at_ref, q_ref, *refs):
    kv_refs = refs[: len(lives)]
    acc_in, m_in, l_in, acc_ref, m_ref, l_ref = refs[len(lives) :]
    rows = q_ref.shape[0]
    live = [f(at_ref) for f in lives]

    def run(blocks_of):
        def body(g):
            k, v_ext = joined(blocks_of(g))
            for h in range(heads):
                cols = span(g, heads * HEAD_SIZE, h * HEAD_SIZE)
                for t in range(0, rows, TILE):
                    at = slice(t, t + TILE)
                    acc, m, l = extend(q_ref, acc_in, m_in, l_in, at, cols, k, v_ext)
                    acc_ref[at, cols] = acc
                    m_ref[at, cols] = m
                    l_ref[at, cols] = l

        each_group(groups, body)

    if len(lives) == 1:
        pl.when(live[0])(lambda: run(lambda g: [pair(kv_refs[0], g)]))
        return
    a, b = live

    def chosen(g):
        ka, va = pair(kv_refs[0], g)
        kb, vb = pair(kv_refs[1], g)
        return [(jnp.where(a, ka, kb), jnp.where(a, va, vb))]

    pl.when(a & b)(lambda: run(lambda g: [pair(r, g) for r in kv_refs]))
    pl.when(a ^ b)(lambda: run(chosen))


def last_kernel(
    heads, groups, alive, at_ref, q_ref, kv_ref, acc_in, m_in, l_in, side_ref, gain_ref, comb_ref, sq_ref
):
    d = HEAD_SIZE
    rows = q_ref.shape[0]
    live = alive(at_ref)
    sq_ref[...] = jnp.zeros_like(sq_ref)

    def run(update):
        def body(g):
            if update:
                k, v_ext = joined([pair(kv_ref, g)])
            for t in range(0, rows, TILE):
                at = slice(t, t + TILE)
                total = jnp.zeros((TILE, d), jnp.float32)
                for h in range(heads):
                    cols = span(g, heads * d, h * d)
                    if update:
                        acc, _, l = extend(q_ref, acc_in, m_in, l_in, at, cols, k, v_ext)
                    else:
                        acc, l = acc_in[at, cols], l_in[at, cols]
                    c = gain_ref[0:1, cols] * (side_ref[at, cols] + acc / l)
                    comb_ref[at, cols] = c
                    total = total + c * c
                sq_ref[:, at] += lax.dot_general(
                    jnp.ones((8, d), jnp.float32), total, nt_dims, precision=exact
                )

        each_group(groups, body)

    pl.when(live)(lambda: run(True))
    pl.when(jnp.logical_not(live))(lambda: run(False))


def weights_of(idx_ref, table_ref):
    entries = table_ref.shape[0]
    rows = idx_ref.shape[0]
    one_hot = (idx_ref[...] == lax.broadcasted_iota(jnp.int32, (rows, entries), 1)).astype(
        jnp.float32
    )
    return jnp.dot(one_hot, table_ref[...], precision=exact, preferred_element_type=jnp.float32)


def intra_kernel(heads, groups, levels, q_ref, k_ref, v_ref, idx_ref, table_ref, out_ref, w_ref):
    d = HEAD_SIZE
    rows = q_ref.shape[0]
    w_ref[...] = weights_of(idx_ref, table_ref)
    row = lax.broadcasted_iota(jnp.int32, (TILE, TILE), 0)
    col = lax.broadcasted_iota(jnp.int32, (TILE, TILE), 1)
    for g in range(groups):
        kv = slice(g * d, (g + 1) * d)
        for h in range(heads):
            head = g * heads + h
            cols = slice(head * d, (head + 1) * d)
            for t in range(0, rows, TILE):
                at = slice(t, t + TILE)
                a = scores_of(q_ref[at, cols], k_ref[: t + TILE, kv]) * (d * rows) ** (-0.5)
                tail = jnp.where(col <= row, a[:, t:], 0.0)
                a = jnp.concatenate([a[:, :t], tail], axis=1) if t else tail
                intra = jnp.dot(
                    a.astype(jnp.bfloat16),
                    v_ref[: t + TILE, kv],
                    preferred_element_type=jnp.float32,
                )
                lane = head * (levels + 1)
                out_ref[at, cols] = w_ref[at, lane : lane + 1] * intra


def readout_kernel(heads, groups, levels, at_ref, q_ref, w_ref, *refs):
    d = HEAD_SIZE
    buckets = refs[:levels]
    side_in, side_ref = refs[levels:]
    rows = q_ref.shape[0]
    here = at_ref[0]
    scales = [
        ((here >> (level - 1)) & 1).astype(jnp.float32) * (d * rows * 2 ** (level - 1)) ** (-0.5)
        for level in range(1, levels + 1)
    ]
    for g in range(groups):
        wide = jnp.concatenate([b[g] for b in buckets], axis=1)
        for h in range(heads):
            head = g * heads + h
            cols = slice(head * d, (head + 1) * d)
            for t in range(0, rows, TILE):
                at = slice(t, t + TILE)
                read = jnp.dot(q_ref[at, cols], wide, preferred_element_type=jnp.float32)
                out = side_in[at, cols]
                for level in range(levels):
                    lane = head * (levels + 1) + level + 1
                    out = out + (w_ref[at, lane : lane + 1] * scales[level]) * read[
                        :, level * d : (level + 1) * d
                    ]
                side_ref[at, cols] = out


def window_kernel(heads, groups, behind, at_ref, q_ref, own_ref, other_ref, *refs):
    d = HEAD_SIZE
    back = refs[:behind]
    side_in, side_ref = refs[behind:]
    rows = q_ref.shape[0]
    here = at_ref[0]
    pick = at_ref[1] != 0

    def run(general):
        def body(g):
            kx, vx = pair(back[-1], g)
            ky, vy = pair(other_ref, g)
            near = (jnp.where(pick, kx, ky), jnp.where(pick, vx, vy))
            k, v_ext = joined([pair(r, g) for r in back[:-1]] + [near, pair(own_ref, g)])
            for h in range(heads):
                cols = span(g, heads * d, h * d)
                for t in range(0, rows, TILE):
                    at = slice(t, t + TILE)
                    start = 0 if general else behind * rows + t - W
                    stop = behind * rows + rows if general else behind * rows + t + TILE
                    s = scores_of(q_ref[at, cols], k[start:stop])
                    if general:
                        at_row = behind * rows + t + lax.broadcasted_iota(jnp.int32, s.shape, 0)
                        at_col = lax.broadcasted_iota(jnp.int32, s.shape, 1)
                        allowed = (at_col <= at_row) & (at_col > at_row - W)
                        allowed = allowed & (at_col >= (behind - here) * rows)
                        s = jnp.where(allowed, s, far_below)
                    else:
                        s = lower_mask(s, True, True)
                    m = jnp.max(s, axis=1, keepdims=True) * UNIT
                    p = jnp.exp2(s * UNIT - m)
                    pv = jnp.dot(
                        p.astype(jnp.bfloat16), v_ext[start:stop], preferred_element_type=jnp.float32
                    )
                    side_ref[at, cols] = side_in[at, cols] + pv[:, :d] / pv[:, d:]

        each_group(groups, body)

    if behind * rows == W:
        pl.when(here >= behind)(lambda: run(False))
        pl.when(here < behind)(lambda: run(True))
    else:
        run(True)


def norm_kernel(columns, parts, comb_ref, *refs):
    sums = refs[0][...]
    for r in refs[1:parts]:
        sums = sums + r[...]
    out_ref = refs[parts]
    g = pl.program_id(0)
    wide = out_ref.shape[1]
    inv = lax.rsqrt(jnp.transpose(sums)[:, 0:1] / columns + 1e-06)
    out_ref[...] = (comb_ref[:, pl.ds(pl.multiple_of(g * wide, LANES), wide)] * inv).astype(
        out_ref.dtype
    )


def per_device(
    q_win,
    k_win,
    v_win,
    q_lin,
    k_lin,
    v_lin,
    level_table,
    level_index,
    q_cross,
    k_shared,
    v_shared,
    head_gain,
):
    d = HEAD_SIZE
    bf16, f32 = jnp.bfloat16, jnp.float32
    rows = q_win.shape[0]
    groups = k_win.shape[1] // d
    heads = q_win.shape[1] // k_win.shape[1]
    count = lax.axis_size("ctx")
    levels = count.bit_length() - 1
    here = lax.axis_index("ctx").astype(jnp.int32)
    behind = -(-W // rows)
    fixed = count == 8 and behind == 2

    full = jax.ShapeDtypeStruct((rows, q_win.shape[1]), f32)
    kv_type = jax.ShapeDtypeStruct((2, rows, k_win.shape[1]), bf16)

    def call(kernel, args, outs, alias=None, scalars=0, work=0.0, limit=24):
        keys = work * rows * rows * groups * heads
        return pl.pallas_call(
            kernel,
            in_specs=[SMEM] * scalars + [VMEM] * (len(args) - scalars),
            out_specs=[VMEM] * len(outs),
            out_shape=outs,
            input_output_aliases=alias or {},
            compiler_params=pltpu.CompilerParams(vmem_limit_bytes=limit << 20),
            cost_estimate=pl.CostEstimate(
                flops=int(4 * keys * d) + 1024, transcendentals=int(keys), bytes_accessed=1 << 20
            ),
        )(*args)

    part = functools.partial
    at = jnp.stack([here, here & 1])
    (shared,) = call(pack_kernel, [k_shared, v_shared], [kv_type])
    (near,) = call(pack_kernel, [k_win, v_win], [kv_type])
    state, half = call(
        state_kernel, [k_lin, v_lin], [jax.ShapeDtypeStruct((groups, d, d), t) for t in (f32, bf16)]
    )
    buckets = []
    for level in range(levels):
        arrived = partner(half, "ctx", level)
        buckets.append(arrived)
        state = state + arrived.astype(f32)
        half = state.astype(bf16)

    index = level_index.reshape(rows, 1)
    table = level_table.reshape(level_table.shape[0], -1)
    gain = jnp.repeat(head_gain, d).reshape(1, -1)

    kernel = lambda f, *extra: part(f, heads, groups, *extra)
    carry = tuple(call(kernel(local_kernel), [q_cross, shared], [full] * 3, work=0.75))
    side, weights = call(
        kernel(intra_kernel, levels),
        [q_lin, k_lin, v_lin, index, table],
        [full, jax.ShapeDtypeStruct((rows, table.shape[1]), f32)],
        work=0.75,
    )

    def piece(lives, kvs, carry, where=at):
        n = len(kvs) + 2
        return tuple(
            call(
                kernel(piece_kernel, lives),
                [where, q_cross, *kvs, *carry],
                [full] * 3,
                alias={n: 0, n + 1: 1, n + 2: 2},
                scalars=1,
                work=len(kvs),
            )
        )

    def windowed(side, back, other, flags):
        return call(
            kernel(window_kernel, behind),
            [flags, q_win, near, other, *back, side],
            [full],
            alias={4 + behind: 0},
            scalars=1,
            work=2.5,
        )[0]

    def read(side):
        return call(
            kernel(readout_kernel, levels),
            [at, q_lin, weights, *buckets, side],
            [full],
            alias={3 + levels: 0},
            scalars=1,
            work=0.75,
        )[0]

    def last(alive, kv, carry, side):
        return call(
            kernel(last_kernel, alive),
            [at, q_cross, kv, *carry, side, gain],
            [full, jax.ShapeDtypeStruct((8, rows), f32)],
            alias={6: 0},
            scalars=1,
            work=1,
        )

    if fixed:

        def straight(steps):
            return lambda ref: ref[0] >= 2 * steps

        def across(steps):
            return lambda ref: (ref[0] >= 2 * steps) if steps else (ref[1] == 1)

        sides = [(2 * i, 2 * i + 1) for i in range(count // 2)]
        z1 = shifted(shared, "ctx", 2)
        x0 = partner(shared, "ctx", 0)
        w2 = shifted(near, "ctx", 2)
        wx = lax.ppermute(near, "ctx", sides)
        z3 = shifted(shared, "ctx", 6)
        z2 = shifted(z1, "ctx", 2)
        x1 = partner(z1, "ctx", 0)
        wb = lax.ppermute(w2, "ctx", [(b, a) for a, b in sides])
        x3 = partner(z3, "ctx", 0)
        x2 = partner(z2, "ctx", 0)
        carry = piece([across(0), straight(1)], [x0, z1], carry)
        carry = piece([across(1), straight(3)], [x1, z3], carry)
        side = windowed(side, [w2, wx], wb, at)
        carry = piece([across(3), straight(2)], [x3, z2], carry)
        side = read(side)
        comb, sq = last(across(2), x2, carry, side)
    else:
        back = [shifted(near, "ctx", step) for step in range(behind, 0, -1)]
        side = read(windowed(side, back, back[-1], jnp.stack([here, here * 0 + 1])))
        every = lax.all_gather(shared, "ctx", axis=0, tiled=False)

        def step(source, carried):
            return piece(
                [lambda ref: ref[1] < ref[0]], [every[source]], carried, jnp.stack([here, source])
            )

        carry = lax.fori_loop(0, count - 2, step, carry)
        comb, sq = last(lambda ref: ref[0] > count - 2, every[count - 2], carry, side)

    members = lax.axis_size("head")
    if members & (members - 1) == 0:
        sums = [sq] + [
            lax.ppermute(sq, "head", [(i, i ^ k) for i in range(members)])
            for k in range(1, members)
        ]
    else:
        sums = [lax.psum(sq, "head")]
    return pl.pallas_call(
        part(norm_kernel, QH * d, len(sums)),
        grid=(groups,),
        in_specs=[VMEM] * (1 + len(sums)),
        out_specs=pl.BlockSpec((rows, heads * d), lambda g: (0, g)),
        out_shape=jax.ShapeDtypeStruct(q_win.shape, bf16),
        compiler_params=pltpu.CompilerParams(vmem_limit_bytes=12 << 20),
        name="norm",
    )(comb, *sums)


def solution(mesh):
    return jax.shard_map(
        per_device,
        mesh=mesh,
        in_specs=(
            P("ctx", "head"),
            P("ctx", "head"),
            P("ctx", "head"),
            P("ctx", "head"),
            P("ctx", "head"),
            P("ctx", "head"),
            P(None, "head", None),
            P("ctx"),
            P("ctx", "head"),
            P("ctx", "head"),
            P("ctx", "head"),
            P("head"),
        ),
        out_specs=P("ctx", "head"),
        check_vma=False,
    )
```

```python
import functools
import math

import jax
import jax.numpy as jnp
from jax import lax
from jax.experimental import pallas as pl
from jax.experimental.pallas import tpu as pltpu
from jax.sharding import PartitionSpec as P


QH = 64
HEAD_SIZE = 128
W = 512
LANES = 128
far_below = -1e30
exact = lax.Precision.HIGHEST
nt_dims = (((1,), (1,)), ((), ()))
tn_dims = (((0,), (0,)), ((), ()))


def shifted(value, axis, steps):
    count = lax.axis_size(axis)
    first, last = (max(0, -steps), min(count, count - steps))
    return lax.ppermute(value, axis, [(source, source + steps) for source in range(first, last)])


def partner(block, axis, apart):
    count = lax.axis_size(axis)
    route = []
    for low in range(count):
        high = low | 1 << apart
        if high != low and high < count:
            route += [(low, high), (high, low)]
    return lax.ppermute(block, axis, route)


def scores_of(q, k):
    return lax.dot_general(q, k, nt_dims, preferred_element_type=jnp.float32)


def with_ones(v):
    return jnp.concatenate([v, jnp.ones(v.shape, v.dtype)], axis=1)


def lower_mask(s, first, last):
    rows = s.shape[0]
    row = lax.broadcasted_iota(jnp.int32, (rows, rows), 0)
    col = lax.broadcasted_iota(jnp.int32, (rows, rows), 1)
    parts = []
    width = s.shape[1]
    if first:
        parts.append(jnp.where(col > row, s[:, :rows], far_below))
    middle = s[:, rows if first else 0 : width - rows if last else width]
    if middle.shape[1]:
        parts.append(middle)
    if last:
        parts.append(jnp.where(col <= row, s[:, width - rows :], far_below))
    return parts[0] if len(parts) == 1 else jnp.concatenate(parts, axis=1)


UNIT = HEAD_SIZE ** (-0.5) * math.log2(math.e)
VMEM = pl.BlockSpec(memory_space=pltpu.VMEM)
SMEM = pl.BlockSpec(memory_space=pltpu.SMEM)
TILE = 128


def span(g, size, at=0):
    return pl.ds(pl.multiple_of(g * size + at, LANES), HEAD_SIZE)


def each_group(groups, body):
    lax.fori_loop(0, groups, lambda g, c: (body(g), c)[1], 0)


def pair(ref, g):
    cols = span(g, HEAD_SIZE)
    return ref[0, :, cols], ref[1, :, cols]


def joined(blocks):
    k = jnp.concatenate([b[0] for b in blocks], axis=0)
    v = jnp.concatenate([b[1] for b in blocks], axis=0)
    return k, with_ones(v)


def fetched(copies, sem):
    started = [pltpu.make_async_copy(src, dst, sem.at[i]) for i, (src, dst) in enumerate(copies)]
    for c in started:
        c.start()
    return started


def pack_kernel(k_ref, v_ref, out_ref, sem):
    for c in fetched([(k_ref, out_ref.at[0]), (v_ref, out_ref.at[1])], sem):
        c.wait()


def local_kernel(heads, groups, q_ref, kv_ref, acc_ref, m_ref, l_ref):
    d = HEAD_SIZE
    rows = q_ref.shape[0]

    def body(g):
        k, v_ext = joined([pair(kv_ref, g)])
        for h in range(heads):
            cols = span(g, heads * d, h * d)
            for t in range(0, rows, TILE):
                at = slice(t, t + TILE)
                s = lower_mask(scores_of(q_ref[at, cols], k[: t + TILE]), False, True)
                m = jnp.max(s, axis=1, keepdims=True) * UNIT
                p = jnp.exp2(s * UNIT - m)
                pv = jnp.dot(
                    p.astype(jnp.bfloat16), v_ext[: t + TILE], preferred_element_type=jnp.float32
                )
                acc_ref[at, cols] = pv[:, :d]
                l_ref[at, cols] = pv[:, d:]
                m_ref[at, cols] = jnp.broadcast_to(m, (TILE, d))

    each_group(groups, body)


def extend(q_ref, acc_ref, m_ref, l_ref, at, cols, k, v_ext):
    d = HEAD_SIZE
    s = scores_of(q_ref[at, cols], k)
    m_old = m_ref[at, cols]
    m = jnp.maximum(jnp.max(s, axis=1, keepdims=True) * UNIT, m_old)
    p = jnp.exp2(s * UNIT - jnp.concatenate([m] * (s.shape[1] // d), axis=1))
    pv = jnp.dot(p.astype(jnp.bfloat16), v_ext, preferred_element_type=jnp.float32)
    fade = jnp.exp2(m_old - m)
    return (
        acc_ref[at, cols] * fade + pv[:, :d],
        m,
        l_ref[at, cols] * fade + pv[:, d:],
    )


def piece_kernel(heads, groups, lives, at_ref, q_ref, *refs):
    kv_refs = refs[: len(lives)]
    acc_in, m_in, l_in, acc_ref, m_ref, l_ref = refs[len(lives) :]
    rows = q_ref.shape[0]
    live = [f(at_ref) for f in lives]

    def run(blocks_of):
        def body(g):
            k, v_ext = joined(blocks_of(g))
            for h in range(heads):
                cols = span(g, heads * HEAD_SIZE, h * HEAD_SIZE)
                for t in range(0, rows, TILE):
                    at = slice(t, t + TILE)
                    acc, m, l = extend(q_ref, acc_in, m_in, l_in, at, cols, k, v_ext)
                    acc_ref[at, cols] = acc
                    m_ref[at, cols] = m
                    l_ref[at, cols] = l

        each_group(groups, body)

    if len(lives) == 1:
        pl.when(live[0])(lambda: run(lambda g: [pair(kv_refs[0], g)]))
        return
    a, b = live

    def chosen(g):
        ka, va = pair(kv_refs[0], g)
        kb, vb = pair(kv_refs[1], g)
        return [(jnp.where(a, ka, kb), jnp.where(a, va, vb))]

    pl.when(a & b)(lambda: run(lambda g: [pair(r, g) for r in kv_refs]))
    pl.when(a ^ b)(lambda: run(chosen))


def last_kernel(
    heads, groups, alive, at_ref, q_ref, kv_ref, acc_in, m_in, l_in, side_ref, gain_ref, comb_ref, sq_ref
):
    d = HEAD_SIZE
    rows = q_ref.shape[0]
    live = alive(at_ref)
    sq_ref[...] = jnp.zeros_like(sq_ref)

    def run(update):
        def body(g):
            if update:
                k, v_ext = joined([pair(kv_ref, g)])
            for t in range(0, rows, TILE):
                at = slice(t, t + TILE)
                total = jnp.zeros((TILE, d), jnp.float32)
                for h in range(heads):
                    cols = span(g, heads * d, h * d)
                    if update:
                        acc, _, l = extend(q_ref, acc_in, m_in, l_in, at, cols, k, v_ext)
                    else:
                        acc, l = acc_in[at, cols], l_in[at, cols]
                    c = gain_ref[0:1, cols] * (side_ref[at, cols] + acc / l)
                    comb_ref[at, cols] = c
                    total = total + c * c
                sq_ref[:, at] += lax.dot_general(
                    jnp.ones((8, d), jnp.float32), total, nt_dims, precision=exact
                )

        each_group(groups, body)

    pl.when(live)(lambda: run(True))
    pl.when(jnp.logical_not(live))(lambda: run(False))


def weights_of(idx_ref, table_ref):
    rows = idx_ref.shape[1]
    entries = table_ref.shape[2]
    one_hot = (idx_ref[...] == lax.broadcasted_iota(jnp.int32, (entries, rows), 0)).astype(
        jnp.float32
    )
    table = jnp.concatenate([table_ref[h] for h in range(table_ref.shape[0])], axis=0)
    return jnp.transpose(
        jnp.dot(table, one_hot, precision=exact, preferred_element_type=jnp.float32)
    )


def intra_kernel(
    heads, groups, levels, k_ref, v_ref, q_ref, idx_ref, table_ref, *refs
):
    out_ref, w_ref, wide_ref, half_ref, kv_ref, sem = refs
    d = HEAD_SIZE
    rows = q_ref.shape[0]
    moves = fetched([(k_ref, kv_ref.at[0]), (v_ref, kv_ref.at[1])], sem)
    w_ref[...] = weights_of(idx_ref, table_ref)
    for c in moves:
        c.wait()
    row = lax.broadcasted_iota(jnp.int32, (TILE, TILE), 0)
    col = lax.broadcasted_iota(jnp.int32, (TILE, TILE), 1)
    for g in range(groups):
        kv = slice(g * d, (g + 1) * d)
        state = lax.dot_general(
            kv_ref[0, :, kv], kv_ref[1, :, kv], tn_dims, preferred_element_type=jnp.float32
        )
        wide_ref[g] = state
        half_ref[g] = state.astype(half_ref.dtype)
        for h in range(heads):
            head = g * heads + h
            cols = slice(head * d, (head + 1) * d)
            for t in range(0, rows, TILE):
                at = slice(t, t + TILE)
                a = scores_of(q_ref[at, cols], kv_ref[0, : t + TILE, kv]) * (d * rows) ** (-0.5)
                tail = jnp.where(col <= row, a[:, t:], 0.0)
                a = jnp.concatenate([a[:, :t], tail], axis=1) if t else tail
                intra = jnp.dot(
                    a.astype(jnp.bfloat16),
                    kv_ref[1, : t + TILE, kv],
                    preferred_element_type=jnp.float32,
                )
                lane = head * (levels + 1)
                out_ref[at, cols] = w_ref[at, lane : lane + 1] * intra


def readout_kernel(heads, groups, levels, at_ref, q_ref, w_ref, *refs):
    d = HEAD_SIZE
    buckets = refs[:levels]
    side_in, side_ref = refs[levels:]
    rows = q_ref.shape[0]
    here = at_ref[0]
    scales = [
        ((here >> (level - 1)) & 1).astype(jnp.float32) * (d * rows * 2 ** (level - 1)) ** (-0.5)
        for level in range(1, levels + 1)
    ]
    for g in range(groups):
        wide = jnp.concatenate([b[g] for b in buckets], axis=1)
        for h in range(heads):
            head = g * heads + h
            cols = slice(head * d, (head + 1) * d)
            for t in range(0, rows, TILE):
                at = slice(t, t + TILE)
                read = jnp.dot(q_ref[at, cols], wide, preferred_element_type=jnp.float32)
                out = side_in[at, cols]
                for level in range(levels):
                    lane = head * (levels + 1) + level + 1
                    out = out + (w_ref[at, lane : lane + 1] * scales[level]) * read[
                        :, level * d : (level + 1) * d
                    ]
                side_ref[at, cols] = out


def window_kernel(heads, groups, behind, picks, at_ref, q_ref, own_ref, other_ref, *refs):
    d = HEAD_SIZE
    back = refs[:behind]
    side_in, side_ref = refs[behind:]
    rows = q_ref.shape[0]
    here = at_ref[0]
    pick = (at_ref[0] & 1) != 0 if picks else True

    def run(general):
        def body(g):
            kx, vx = pair(back[-1], g)
            ky, vy = pair(other_ref, g)
            near = (jnp.where(pick, kx, ky), jnp.where(pick, vx, vy)) if picks else (kx, vx)
            k, v_ext = joined([pair(r, g) for r in back[:-1]] + [near, pair(own_ref, g)])
            for h in range(heads):
                cols = span(g, heads * d, h * d)
                for t in range(0, rows, TILE):
                    at = slice(t, t + TILE)
                    start = 0 if general else behind * rows + t - W
                    stop = behind * rows + rows if general else behind * rows + t + TILE
                    s = scores_of(q_ref[at, cols], k[start:stop])
                    if general:
                        at_row = behind * rows + t + lax.broadcasted_iota(jnp.int32, s.shape, 0)
                        at_col = lax.broadcasted_iota(jnp.int32, s.shape, 1)
                        allowed = (at_col <= at_row) & (at_col > at_row - W)
                        allowed = allowed & (at_col >= (behind - here) * rows)
                        s = jnp.where(allowed, s, far_below)
                    else:
                        s = lower_mask(s, True, True)
                    m = jnp.max(s, axis=1, keepdims=True) * UNIT
                    p = jnp.exp2(s * UNIT - m)
                    pv = jnp.dot(
                        p.astype(jnp.bfloat16), v_ext[start:stop], preferred_element_type=jnp.float32
                    )
                    side_ref[at, cols] = side_in[at, cols] + pv[:, :d] / pv[:, d:]

        each_group(groups, body)

    if behind * rows == W:
        pl.when(here >= behind)(lambda: run(False))
        pl.when(here < behind)(lambda: run(True))
    else:
        run(True)


def norm_kernel(columns, parts, comb_ref, *refs):
    sums = refs[0][...]
    for r in refs[1:parts]:
        sums = sums + r[...]
    out_ref = refs[parts]
    g = pl.program_id(0)
    wide = out_ref.shape[1]
    inv = lax.rsqrt(jnp.transpose(sums)[:, 0:1] / columns + 1e-06)
    out_ref[...] = (comb_ref[:, pl.ds(pl.multiple_of(g * wide, LANES), wide)] * inv).astype(
        out_ref.dtype
    )


def per_device(
    q_win,
    k_win,
    v_win,
    q_lin,
    k_lin,
    v_lin,
    level_table,
    level_index,
    q_cross,
    k_shared,
    v_shared,
    head_gain,
):
    d = HEAD_SIZE
    bf16, f32 = jnp.bfloat16, jnp.float32
    rows = q_win.shape[0]
    groups = k_win.shape[1] // d
    heads = q_win.shape[1] // k_win.shape[1]
    count = lax.axis_size("ctx")
    levels = count.bit_length() - 1
    here = lax.axis_index("ctx").astype(jnp.int32)
    behind = -(-W // rows)
    fixed = count == 8 and behind == 2

    full = jax.ShapeDtypeStruct((rows, q_win.shape[1]), f32)
    kv_type = jax.ShapeDtypeStruct((2, rows, k_win.shape[1]), bf16)

    def call(kernel, args, outs, alias=None, scalars=0, work=0.0, raw=0, copies=0, scratch=(), limit=24):
        keys = work * rows * rows * groups * heads
        return pl.pallas_call(
            kernel,
            in_specs=[SMEM] * scalars
            + [pl.BlockSpec(memory_space=pltpu.HBM)] * raw
            + [VMEM] * (len(args) - scalars - raw),
            out_specs=[VMEM] * len(outs),
            out_shape=outs,
            scratch_shapes=[*scratch] + [pltpu.SemaphoreType.DMA((copies,))] * (copies > 0),
            input_output_aliases=alias or {},
            compiler_params=pltpu.CompilerParams(vmem_limit_bytes=limit << 20),
            cost_estimate=pl.CostEstimate(
                flops=int(4 * keys * d) + 1024, transcendentals=int(keys), bytes_accessed=1 << 20
            ),
        )(*args)

    def on_chip(*blocks):
        return [pltpu.with_memory_space_constraint(b, pltpu.VMEM) for b in blocks]

    part = functools.partial
    at = here.reshape(1)
    k_shared, v_shared, k_win, v_win, k_lin, v_lin = (
        pltpu.with_memory_space_constraint(x, pltpu.HBM)
        for x in (k_shared, v_shared, k_win, v_win, k_lin, v_lin)
    )
    (shared,) = call(pack_kernel, [k_shared, v_shared], [kv_type], raw=2, copies=2, limit=4)
    (near,) = call(pack_kernel, [k_win, v_win], [kv_type], raw=2, copies=2, limit=4)
    index = level_index.reshape(1, rows)
    table = level_table.transpose(1, 2, 0)
    kernel = lambda f, *extra: part(f, heads, groups, *extra)
    side, weights, state, half = call(
        kernel(intra_kernel, levels),
        [k_lin, v_lin, q_lin, index, table],
        [full, jax.ShapeDtypeStruct((rows, table.shape[0] * table.shape[1]), f32)]
        + [jax.ShapeDtypeStruct((groups, d, d), t) for t in (f32, bf16)],
        raw=2,
        copies=2,
        scratch=[pltpu.VMEM(kv_type.shape, bf16)],
        work=0.75,
    )
    buckets = []
    for level in range(levels):
        arrived = partner(half, "ctx", level)
        buckets.append(arrived)
        state = state + arrived.astype(f32)
        half = state.astype(bf16)

    gain = jnp.repeat(head_gain, d).reshape(1, -1)

    carry = tuple(call(kernel(local_kernel), [q_cross, shared], [full] * 3, work=0.75))

    def piece(lives, kvs, carry, where=at):
        n = len(kvs) + 2
        return tuple(
            call(
                kernel(piece_kernel, lives),
                [where, q_cross, *kvs, *carry],
                [full] * 3,
                alias={n: 0, n + 1: 1, n + 2: 2},
                scalars=1,
                work=len(kvs),
            )
        )

    def windowed(side, back, other, picks):
        return call(
            kernel(window_kernel, behind, picks),
            [at, q_win, near, other, *back, side],
            [full],
            alias={4 + behind: 0},
            scalars=1,
            work=2.5,
        )[0]

    def read(side):
        return call(
            kernel(readout_kernel, levels),
            [at, q_lin, weights, *buckets, side],
            [full],
            alias={3 + levels: 0},
            scalars=1,
            work=0.75,
        )[0]

    def last(alive, kv, carry, side):
        return call(
            kernel(last_kernel, alive),
            [at, q_cross, kv, *carry, side, gain],
            [full, jax.ShapeDtypeStruct((8, rows), f32)],
            alias={6: 0},
            scalars=1,
            work=1,
        )

    if fixed:

        def straight(steps):
            return lambda ref: ref[0] >= 2 * steps

        def across(steps):
            return lambda ref: (ref[0] >= 2 * steps) if steps else ((ref[0] & 1) == 1)

        sides = [(2 * i, 2 * i + 1) for i in range(count // 2)]
        z1 = shifted(shared, "ctx", 2)
        x0 = partner(shared, "ctx", 0)
        w2 = shifted(near, "ctx", 2)
        wx = lax.ppermute(near, "ctx", sides)
        z3 = shifted(shared, "ctx", 6)
        z2 = shifted(z1, "ctx", 2)
        x1 = partner(z1, "ctx", 0)
        wb = lax.ppermute(w2, "ctx", [(b, a) for a, b in sides])
        x3 = partner(z3, "ctx", 0)
        x2 = partner(z2, "ctx", 0)
        carry = piece([across(0), straight(1)], on_chip(x0, z1), carry)
        carry = piece([across(1), straight(3)], on_chip(x1, z3), carry)
        side = windowed(side, on_chip(w2, wx), *on_chip(wb), True)
        carry = piece([across(3), straight(2)], on_chip(x3, z2), carry)
        side = read(side)
        comb, sq = last(across(2), x2, carry, side)
    else:
        back = [shifted(near, "ctx", step) for step in range(behind, 0, -1)]
        side = read(windowed(side, back, back[-1], False))
        every = lax.all_gather(shared, "ctx", axis=0, tiled=False)

        def step(source, carried):
            return piece(
                [lambda ref: ref[1] < ref[0]], [every[source]], carried, jnp.stack([here, source])
            )

        carry = lax.fori_loop(0, count - 2, step, carry)
        comb, sq = last(lambda ref: ref[0] > count - 2, every[count - 2], carry, side)

    members = lax.axis_size("head")
    if members & (members - 1) == 0:
        sums = [sq] + [
            lax.ppermute(sq, "head", [(i, i ^ k) for i in range(members)])
            for k in range(1, members)
        ]
    else:
        sums = [lax.psum(sq, "head")]
    return pl.pallas_call(
        part(norm_kernel, QH * d, len(sums)),
        grid=(groups,),
        in_specs=[VMEM] * (1 + len(sums)),
        out_specs=pl.BlockSpec((rows, heads * d), lambda g: (0, g)),
        out_shape=jax.ShapeDtypeStruct(q_win.shape, bf16),
        compiler_params=pltpu.CompilerParams(vmem_limit_bytes=12 << 20),
        name="norm",
    )(comb, *sums)


def solution(mesh):
    return jax.shard_map(
        per_device,
        mesh=mesh,
        in_specs=(
            P("ctx", "head"),
            P("ctx", "head"),
            P("ctx", "head"),
            P("ctx", "head"),
            P("ctx", "head"),
            P("ctx", "head"),
            P(None, "head", None),
            P("ctx"),
            P("ctx", "head"),
            P("ctx", "head"),
            P("ctx", "head"),
            P("head"),
        ),
        out_specs=P("ctx", "head"),
        check_vma=False,
    )
```

```python
import functools
import math

import jax
import jax.numpy as jnp
from jax import lax
from jax.experimental import pallas as pl
from jax.experimental.pallas import tpu as pltpu
from jax.sharding import PartitionSpec as P


QH = 64
HEAD_SIZE = 128
W = 512
LANES = 128
far_below = -1e30
exact = lax.Precision.HIGHEST
nt_dims = (((1,), (1,)), ((), ()))
tn_dims = (((0,), (0,)), ((), ()))


def shifted(value, axis, steps):
    count = lax.axis_size(axis)
    first, last = (max(0, -steps), min(count, count - steps))
    return lax.ppermute(value, axis, [(source, source + steps) for source in range(first, last)])


def partner(block, axis, apart):
    count = lax.axis_size(axis)
    route = []
    for low in range(count):
        high = low | 1 << apart
        if high != low and high < count:
            route += [(low, high), (high, low)]
    return lax.ppermute(block, axis, route)


def scores_of(q, k):
    return lax.dot_general(q, k, nt_dims, preferred_element_type=jnp.float32)


def with_ones(v):
    return jnp.concatenate([v, jnp.ones(v.shape, v.dtype)], axis=1)


def lower_mask(s, first, last):
    rows = s.shape[0]
    row = lax.broadcasted_iota(jnp.int32, (rows, rows), 0)
    col = lax.broadcasted_iota(jnp.int32, (rows, rows), 1)
    parts = []
    width = s.shape[1]
    if first:
        parts.append(jnp.where(col > row, s[:, :rows], far_below))
    middle = s[:, rows if first else 0 : width - rows if last else width]
    if middle.shape[1]:
        parts.append(middle)
    if last:
        parts.append(jnp.where(col <= row, s[:, width - rows :], far_below))
    return parts[0] if len(parts) == 1 else jnp.concatenate(parts, axis=1)


UNIT = HEAD_SIZE ** (-0.5) * math.log2(math.e)
VMEM = pl.BlockSpec(memory_space=pltpu.VMEM)
SMEM = pl.BlockSpec(memory_space=pltpu.SMEM)
TILE = 256


def span(g, size, at=0):
    if isinstance(g, int):
        return slice(g * size + at, g * size + at + HEAD_SIZE)
    return pl.ds(pl.multiple_of(g * size + at, LANES), HEAD_SIZE)


def each_group(groups, body, unrolled=True):
    if unrolled:
        for g in range(groups):
            body(g)
    else:
        lax.fori_loop(0, groups, lambda g, c: (body(g), c)[1], 0)


def pair(ref, g):
    cols = span(g, HEAD_SIZE)
    return ref[0, :, cols], ref[1, :, cols]


def joined(blocks):
    k = jnp.concatenate([b[0] for b in blocks], axis=0)
    v = jnp.concatenate([b[1] for b in blocks], axis=0)
    return k, with_ones(v)


def fetched(copies, sem):
    started = [pltpu.make_async_copy(src, dst, sem.at[i]) for i, (src, dst) in enumerate(copies)]
    for c in started:
        c.start()
    return started


def pack_kernel(ks_ref, vs_ref, kw_ref, vw_ref, shared_ref, near_ref, sem):
    for c in fetched(
        [
            (ks_ref, shared_ref.at[0]),
            (vs_ref, shared_ref.at[1]),
            (kw_ref, near_ref.at[0]),
            (vw_ref, near_ref.at[1]),
        ],
        sem,
    ):
        c.wait()


class Blocks:
    def __init__(self, refs, raw, buf, sem):
        self.refs, self.raw, self.buf, self.sem = refs, raw, buf, sem

    def move(self, i, g):
        n = self.raw.index(i)
        cols = span(g, HEAD_SIZE)
        return pltpu.make_async_copy(
            self.refs[i].at[:, :, cols], self.buf.at[n, :, :, cols], self.sem.at[n, g]
        )

    def start(self, groups):
        for g in range(groups):
            for i in self.raw:
                self.move(i, g).start()

    def ready(self, g):
        for i in self.raw:
            self.move(i, g).wait()

    def __getitem__(self, i):
        return self.buf.at[self.raw.index(i)] if i in self.raw else self.refs[i]


def local_kernel(heads, groups, kv_raw, q_ref, acc_ref, m_ref, l_ref, buf, sem):
    held_ref = (acc_ref, m_ref, l_ref)
    d = HEAD_SIZE
    rows = q_ref.shape[0]
    blocks = Blocks([kv_raw], [0], buf, sem)
    blocks.start(groups)

    def body(g):
        blocks.ready(g)
        k, v_ext = joined([pair(blocks[0], g)])
        for h in range(heads):
            cols = span(g, heads * d, h * d)
            for t in range(0, rows, TILE):
                at = slice(t, t + TILE)
                s = lower_mask(scores_of(q_ref[at, cols], k[: t + TILE]), False, True)
                m = top_of(s)
                pv = weighed(s, m, v_ext[: t + TILE])
                held_ref[0][at, cols] = pv[:, :d]
                held_ref[1][at, cols] = m
                held_ref[2][at, cols] = pv[:, d:]

    each_group(groups, body)


def top_of(s):
    return jnp.broadcast_to(jnp.max(s, axis=1, keepdims=True), (s.shape[0], LANES)) * UNIT


def weighed(s, m, v_ext):
    p = jnp.exp2(s * UNIT - jnp.concatenate([m] * (s.shape[1] // LANES), axis=1))
    return jnp.dot(p.astype(jnp.bfloat16), v_ext, preferred_element_type=jnp.float32)


def extend(q_ref, held_ref, at, cols, k, v_ext):
    d = HEAD_SIZE
    s = scores_of(q_ref[at, cols], k)
    m_old = held_ref[1][at, cols]
    m = jnp.maximum(top_of(s), m_old)
    pv = weighed(s, m, v_ext)
    fade = jnp.exp2(m_old - m)
    return (
        held_ref[0][at, cols] * fade + pv[:, :d],
        m,
        held_ref[2][at, cols] * fade + pv[:, d:],
    )


def piece_kernel(heads, groups, lives, raw, at_ref, *refs):
    n = len(lives)
    kv_refs, q_ref = refs[:n], refs[n]
    held_in, held_ref = refs[n + 1 : n + 4], refs[n + 4 : n + 7]
    blocks = Blocks(kv_refs, raw, *(refs[n + 7 :] or (None, None)))
    rows = q_ref.shape[0]
    live = [f(at_ref) for f in lives]

    def run(blocks_of, unrolled=True):
        blocks.start(groups)

        def body(g):
            blocks.ready(g)
            k, v_ext = joined(blocks_of(g))
            for h in range(heads):
                cols = span(g, heads * HEAD_SIZE, h * HEAD_SIZE)
                for t in range(0, rows, TILE):
                    at = slice(t, t + TILE)
                    acc, m, l = extend(q_ref, held_in, at, cols, k, v_ext)
                    held_ref[0][at, cols] = acc
                    held_ref[1][at, cols] = m
                    held_ref[2][at, cols] = l

        each_group(groups, body, unrolled)

    if n == 1:
        pl.when(live[0])(lambda: run(lambda g: [pair(blocks[0], g)]))
        return
    a, b = live

    def chosen(g):
        ka, va = pair(blocks[0], g)
        kb, vb = pair(blocks[1], g)
        return [(jnp.where(a, ka, kb), jnp.where(a, va, vb))]

    pl.when(a & b)(lambda: run(lambda g: [pair(blocks[i], g) for i in range(n)]))
    pl.when(a ^ b)(lambda: run(chosen, False))


def last_kernel(
    heads, groups, alive, at_ref, q_ref, kv_ref, acc_in, m_in, l_in, side_ref, gain_ref, comb_ref, sq_ref, sum_ref
):
    held_in = (acc_in, m_in, l_in)
    d = HEAD_SIZE
    rows = q_ref.shape[0]
    live = alive(at_ref)
    sum_ref[...] = jnp.zeros_like(sum_ref)

    def run(update):
        def body(g):
            if update:
                k, v_ext = joined([pair(kv_ref, g)])
            for t in range(0, rows, TILE):
                at = slice(t, t + TILE)
                total = jnp.zeros((TILE, d), jnp.float32)
                for h in range(heads):
                    cols = span(g, heads * d, h * d)
                    if update:
                        acc, _, l = extend(q_ref, held_in, at, cols, k, v_ext)
                    else:
                        acc, l = held_in[0][at, cols], held_in[2][at, cols]
                    c = gain_ref[0:1, cols] * (side_ref[at, cols] + acc * pl.reciprocal(l))
                    comb_ref[at, cols] = c
                    total = total + c * c
                sum_ref[at] += total

        each_group(groups, body, update)

    pl.when(live)(lambda: run(True))
    pl.when(jnp.logical_not(live))(lambda: run(False))
    sq_ref[...] = lax.dot_general(
        jnp.ones((8, d), jnp.float32), sum_ref[...], nt_dims, precision=exact
    )


def weights_of(idx_ref, table_ref):
    rows = idx_ref.shape[1]
    entries = table_ref.shape[2]
    one_hot = (idx_ref[...] == lax.broadcasted_iota(jnp.int32, (entries, rows), 0)).astype(
        jnp.float32
    )
    table = jnp.concatenate([table_ref[h] for h in range(table_ref.shape[0])], axis=0)
    return jnp.transpose(
        jnp.dot(table, one_hot, precision=exact, preferred_element_type=jnp.float32)
    )


def intra_kernel(
    heads, groups, levels, k_ref, v_ref, q_ref, idx_ref, table_ref, *refs
):
    out_ref, wide_ref, half_ref, kv_ref, q_buf, idx_buf, table_buf, sem = refs
    d = HEAD_SIZE
    rows = q_ref.shape[0]
    moves = fetched(
        [
            (k_ref, kv_ref.at[0]),
            (v_ref, kv_ref.at[1]),
            (idx_ref, idx_buf),
            (table_ref, table_buf),
            (q_ref, q_buf),
        ],
        sem,
    )
    for c in moves:
        c.wait()
    q_ref = q_buf
    weights = weights_of(idx_buf, table_buf)
    base = groups * heads * d
    out_ref[:, base : base + weights.shape[1]] = weights
    row = lax.broadcasted_iota(jnp.int32, (TILE, TILE), 0)
    col = lax.broadcasted_iota(jnp.int32, (TILE, TILE), 1)
    for g in range(groups):
        kv = slice(g * d, (g + 1) * d)
        state = lax.dot_general(
            kv_ref[0, :, kv], kv_ref[1, :, kv], tn_dims, preferred_element_type=jnp.float32
        )
        wide_ref[g] = state
        half_ref[g] = state.astype(half_ref.dtype)
        for h in range(heads):
            head = g * heads + h
            cols = slice(head * d, (head + 1) * d)
            for t in range(0, rows, TILE):
                at = slice(t, t + TILE)
                a = scores_of(q_ref[at, cols], kv_ref[0, : t + TILE, kv]) * (d * rows) ** (-0.5)
                tail = jnp.where(col <= row, a[:, t:], 0.0)
                a = jnp.concatenate([a[:, :t], tail], axis=1) if t else tail
                intra = jnp.dot(
                    a.astype(jnp.bfloat16),
                    kv_ref[1, : t + TILE, kv],
                    preferred_element_type=jnp.float32,
                )
                lane = head * (levels + 1)
                out_ref[at, cols] = weights[at, lane : lane + 1] * intra


def readout_kernel(heads, groups, levels, at_ref, q_ref, *refs):
    d = HEAD_SIZE
    buckets = refs[:levels]
    side_in, side_ref = refs[levels:]
    rows = q_ref.shape[0]
    here = at_ref[0]
    scales = [
        ((here >> (level - 1)) & 1).astype(jnp.float32) * (d * rows * 2 ** (level - 1)) ** (-0.5)
        for level in range(1, levels + 1)
    ]
    for g in range(groups):
        wide = jnp.concatenate([b[g] for b in buckets], axis=1)
        for h in range(heads):
            head = g * heads + h
            cols = slice(head * d, (head + 1) * d)
            for t in range(0, rows, TILE):
                at = slice(t, t + TILE)
                read = jnp.dot(q_ref[at, cols], wide, preferred_element_type=jnp.float32)
                out = side_in[at, cols]
                for level in range(levels):
                    lane = (groups * heads) * d + head * (levels + 1) + level + 1
                    out = out + (side_in[at, lane : lane + 1] * scales[level]) * read[
                        :, level * d : (level + 1) * d
                    ]
                side_ref[at, cols] = out


def window_kernel(heads, groups, behind, picks, raw, at_ref, *refs):
    d = HEAD_SIZE
    n = behind + 2
    blocks = Blocks(refs[:n], raw, *refs[n + 3 :])
    q_ref, side_in, side_ref = refs[n : n + 3]
    rows = q_ref.shape[0]
    here = at_ref[0]
    pick = (at_ref[0] & 1) != 0 if picks else True
    blocks.start(groups)

    def run(general):
        def body(g):
            blocks.ready(g)
            kx, vx = pair(blocks[behind - 1], g)
            ky, vy = pair(blocks[behind + 1], g)
            near = (jnp.where(pick, kx, ky), jnp.where(pick, vx, vy)) if picks else (kx, vx)
            k, v_ext = joined(
                [pair(blocks[i], g) for i in range(behind - 1)] + [near, pair(blocks[behind], g)]
            )
            for h in range(heads):
                cols = span(g, heads * d, h * d)
                for t in range(0, rows, TILE):
                    at = slice(t, t + TILE)
                    start = 0 if general else behind * rows + t - W
                    stop = behind * rows + rows if general else behind * rows + t + TILE
                    s = scores_of(q_ref[at, cols], k[start:stop])
                    if general:
                        at_row = behind * rows + t + lax.broadcasted_iota(jnp.int32, s.shape, 0)
                        at_col = lax.broadcasted_iota(jnp.int32, s.shape, 1)
                        allowed = (at_col <= at_row) & (at_col > at_row - W)
                        allowed = allowed & (at_col >= (behind - here) * rows)
                        s = jnp.where(allowed, s, far_below)
                    else:
                        s = lower_mask(s, True, True)
                    pv = weighed(s, top_of(s), v_ext[start:stop])
                    side_ref[at, cols] = side_in[at, cols] + pv[:, :d] * pl.reciprocal(pv[:, d:])

        each_group(groups, body, not general)

    if behind * rows == W:
        pl.when(here >= behind)(lambda: run(False))
        pl.when(here < behind)(lambda: run(True))
    else:
        run(True)


def norm_kernel(columns, parts, comb_ref, *refs):
    sums = refs[0][...]
    for r in refs[1:parts]:
        sums = sums + r[...]
    out_ref = refs[parts]
    g = pl.program_id(0)
    wide = out_ref.shape[1]
    inv = lax.rsqrt(jnp.transpose(sums)[:, 0:1] / columns + 1e-06)
    out_ref[...] = (comb_ref[:, pl.ds(pl.multiple_of(g * wide, LANES), wide)] * inv).astype(
        out_ref.dtype
    )


def per_device(
    q_win,
    k_win,
    v_win,
    q_lin,
    k_lin,
    v_lin,
    level_table,
    level_index,
    q_cross,
    k_shared,
    v_shared,
    head_gain,
):
    d = HEAD_SIZE
    bf16, f32 = jnp.bfloat16, jnp.float32
    rows = q_win.shape[0]
    groups = k_win.shape[1] // d
    heads = q_win.shape[1] // k_win.shape[1]
    count = lax.axis_size("ctx")
    levels = count.bit_length() - 1
    here = lax.axis_index("ctx").astype(jnp.int32)
    behind = -(-W // rows)
    fixed = count == 8 and behind == 2

    full = jax.ShapeDtypeStruct((rows, q_win.shape[1]), f32)
    kv_type = jax.ShapeDtypeStruct((2, rows, k_win.shape[1]), bf16)

    def call(kernel, args, outs, alias=None, scalars=0, raw=0, scratch=(), limit=10 if fixed else 28):
        return pl.pallas_call(
            kernel,
            in_specs=[SMEM] * scalars
            + [pl.BlockSpec(memory_space=pltpu.HBM)] * raw
            + [VMEM] * (len(args) - scalars - raw),
            out_specs=[VMEM] * len(outs),
            out_shape=outs,
            scratch_shapes=scratch,
            input_output_aliases=alias or {},
            compiler_params=pltpu.CompilerParams(vmem_limit_bytes=limit << 20),
            cost_estimate=pl.CostEstimate(flops=1024, transcendentals=0, bytes_accessed=1024),
        )(*args)

    def in_hbm(*blocks):
        return [pltpu.with_memory_space_constraint(b, pltpu.HBM) for b in blocks]

    def buffers(n):
        return [
            pltpu.VMEM((n,) + kv_type.shape, bf16),
            pltpu.SemaphoreType.DMA((n, groups)),
        ]

    part = functools.partial
    at = here.reshape(1)
    shared, near = call(
        pack_kernel,
        in_hbm(k_shared, v_shared, k_win, v_win),
        [kv_type] * 2,
        raw=4,
        scratch=[pltpu.SemaphoreType.DMA((4,))],
        limit=4,
    )
    index = level_index.reshape(1, rows)
    table = level_table.transpose(1, 2, 0)
    kernel = lambda f, *extra: part(f, heads, groups, *extra)
    per = table.shape[0] * table.shape[1]
    side_type = jax.ShapeDtypeStruct((rows, full.shape[1] + -(-per // LANES) * LANES), f32)
    side, state, half = call(
        kernel(intra_kernel, levels),
        in_hbm(k_lin, v_lin, q_lin, index, table),
        [side_type]
        + [jax.ShapeDtypeStruct((groups, d, d), t) for t in (f32, bf16)],
        raw=5,
        scratch=[
            pltpu.VMEM(kv_type.shape, bf16),
            pltpu.VMEM(q_lin.shape, bf16),
            pltpu.VMEM(index.shape, index.dtype),
            pltpu.VMEM(table.shape, f32),
            pltpu.SemaphoreType.DMA((5,)),
        ],
    )
    buckets = []
    for level in range(levels):
        arrived = partner(half, "ctx", level)
        buckets.append(arrived)
        state = state + arrived.astype(f32)
        half = state.astype(bf16)

    gain = jnp.repeat(head_gain, d).reshape(1, -1)

    carry = call(
        kernel(local_kernel), [*in_hbm(shared), q_cross], [full] * 3, raw=1, scratch=buffers(1)
    )

    def piece(lives, raw, kvs, carry, where=at):
        n = len(kvs) + 2
        kvs = in_hbm(*kvs[:raw]) + list(kvs[raw:])
        return call(
            kernel(piece_kernel, lives, list(range(raw))),
            [where, *kvs, q_cross, *carry],
            [full] * 3,
            alias={n: 0, n + 1: 1, n + 2: 2},
            scalars=1,
            raw=raw,
            scratch=buffers(raw) if raw else [],
        )

    def windowed(side, back, other, picks):
        raw = behind + 1
        return call(
            kernel(window_kernel, behind, picks, list(range(raw))),
            [at, *in_hbm(*back, near), other, q_win, side],
            [side_type],
            alias={4 + behind: 0},
            scalars=1,
            raw=raw,
            scratch=buffers(raw),
        )[0]

    def read(side):
        return call(
            kernel(readout_kernel, levels),
            [at, q_lin, *buckets, side],
            [side_type],
            alias={2 + levels: 0},
            scalars=1,
        )[0]

    def last(alive, kv, carry, side):
        return call(
            kernel(last_kernel, alive),
            [at, q_cross, kv, *carry, side, gain],
            [full, jax.ShapeDtypeStruct((8, rows), f32)],
            scalars=1,
            scratch=[pltpu.VMEM((rows, d), f32)],
        )

    if fixed:

        def straight(steps):
            return lambda ref: ref[0] >= 2 * steps

        def across(steps):
            return lambda ref: (ref[0] >= 2 * steps) if steps else ((ref[0] & 1) == 1)

        sides = [(2 * i, 2 * i + 1) for i in range(count // 2)]
        z1 = shifted(shared, "ctx", 2)
        x0 = partner(shared, "ctx", 0)
        w2 = shifted(near, "ctx", 2)
        wx = lax.ppermute(near, "ctx", sides)
        z3 = shifted(shared, "ctx", 6)
        z2 = shifted(z1, "ctx", 2)
        x1 = partner(z1, "ctx", 0)
        wb = lax.ppermute(w2, "ctx", [(b, a) for a, b in sides])
        x3 = partner(z3, "ctx", 0)
        x2 = partner(z2, "ctx", 0)
        carry = piece([across(0), straight(1)], 2, [x0, z1], carry)
        carry = piece([straight(3), across(1)], 2, [z3, x1], carry)
        side = windowed(side, [w2, wx], wb, True)
        carry = piece([across(3), straight(2)], 0, [x3, z2], carry)
        side = read(side)
        comb, sq = last(across(2), x2, carry, side)
    else:
        back = [shifted(near, "ctx", step) for step in range(behind, 0, -1)]
        side = read(windowed(side, back, back[-1], False))
        every = lax.all_gather(shared, "ctx", axis=0, tiled=False)

        def step(source, carried):
            return piece(
                [lambda ref: ref[1] < ref[0]],
                0,
                [every[source]],
                carried,
                jnp.stack([here, source]),
            )

        carry = lax.fori_loop(0, count - 2, step, carry)
        comb, sq = last(lambda ref: ref[0] > count - 2, every[count - 2], carry, side)

    members = lax.axis_size("head")
    if members & (members - 1) == 0:
        sums = [sq] + [
            lax.ppermute(sq, "head", [(i, i ^ k) for i in range(members)])
            for k in range(1, members)
        ]
    else:
        sums = [lax.psum(sq, "head")]
    return pl.pallas_call(
        part(norm_kernel, QH * d, len(sums)),
        grid=(groups,),
        in_specs=[VMEM] * (1 + len(sums)),
        out_specs=pl.BlockSpec((rows, heads * d), lambda g: (0, g)),
        out_shape=jax.ShapeDtypeStruct(q_win.shape, bf16),
        compiler_params=pltpu.CompilerParams(vmem_limit_bytes=12 << 20),
        name="norm",
    )(comb, *sums)


def solution(mesh):
    step = jax.shard_map(
        per_device,
        mesh=mesh,
        in_specs=(
            P("ctx", "head"),
            P("ctx", "head"),
            P("ctx", "head"),
            P("ctx", "head"),
            P("ctx", "head"),
            P("ctx", "head"),
            P(None, "head", None),
            P("ctx"),
            P("ctx", "head"),
            P("ctx", "head"),
            P("ctx", "head"),
            P("head"),
        ),
        out_specs=P("ctx", "head"),
        check_vma=False,
    )
    if mesh.shape["ctx"] != 8:
        return step
    return step
```
